128 devices in a mesh: tm: 16 (over z, y_hi, core), space: 8 (over x, y_lo).
Axes of the slice: x: 4, y: 4 (y_hi: 2, y_lo: 2; y = y_hi * 2 + y_lo), z: 4, core: 2. Of those that a mesh axis runs over, the one named last changes fastest.
Arguments:
- tokens: bfloat16 [1, 32, 1024, 1536], P(None, 'tm', 'space'), may hold values from -6 to 6
- grad_out: bfloat16 [1, 32, 1024, 1536], P(None, 'tm', 'space'), may hold values from -6 to 6
- temporal_query: bfloat16 [1536, 768], replicated
- temporal_key: bfloat16 [1536, 768], replicated
- temporal_value: bfloat16 [1536, 768], replicated, may hold values from -0.15625 to 0.15625
- temporal_out: bfloat16 [768, 1536], replicated, may hold values from -0.21875 to 0.21875
- spatial_query: bfloat16 [1536, 768], replicated
- spatial_key: bfloat16 [1536, 768], replicated
- spatial_value: bfloat16 [1536, 768], replicated, may hold values from -0.15625 to 0.15625
- spatial_out: bfloat16 [768, 1536], replicated, may hold values from -0.21875 to 0.21875
Outputs:
- grad_in: bfloat16 [1, 32, 1024, 1536], P(None, 'tm', 'space')
The draws below stay inside these ranges and needn't reach their ends.
All inputs are finite; a program needn't handle non-finite values.
Results may differ from the reference program's by a relative error of at most 0.025.
Values may be sent and summed in bfloat16 or wider, within the bound.
A program may use at most 192 MiB of HBM per device.

```python
import jax
import jax.numpy as jnp
from jax import lax

D = 1536
HEADS = 6
HD = 128
TIMES = 32
PATCHES = 1024
BATCH = 1
HW = 768


def clipped_normal(key, salt):
    fresh = jax.random.normal(jax.random.fold_in(key, salt), (D, HEADS * HD), jnp.float32)
    return jnp.clip(fresh, -6.0, 6.0)


def key_like(key, salt):
    return clipped_normal(key, salt) * (2.0 / D) ** 0.5


def query_like(key, salt):
    scale_factor = (2.0 / D) ** 0.5
    fresh = clipped_normal(key, salt + 1)
    return fresh * scale_factor


def draw_temporal_query(key, part):
    return query_like(key, 101).astype(jnp.bfloat16)


def draw_temporal_key(key, part):
    return key_like(key, 101).astype(jnp.bfloat16)


def draw_spatial_query(key, part):
    return query_like(key, 202).astype(jnp.bfloat16)


def draw_spatial_key(key, part):
    return key_like(key, 202).astype(jnp.bfloat16)


def block_levels(own_key, shape, cuts, least, largest):
    loudness = 1.0
    for dim, shards_of in cuts:
        heights = jax.random.uniform(jax.random.fold_in(jax.random.fold_in(own_key, 6), dim), (shards_of,), jnp.float32, least / len(cuts), largest / len(cuts))
        loudness = loudness * jnp.repeat(jnp.exp(heights), shape[dim] // shards_of).reshape((-1,) + (1,) * (len(shape) - 1 - dim))
    return loudness


def gaussian(stream_key, dims, deviation, most, shards=(), dtype=jnp.bfloat16):
    drawn = jax.random.normal(stream_key, dims, jnp.float32) * deviation
    if len(shards) > 0:
        drawn = block_levels(stream_key, dims, shards, -0.22, 0.18) * drawn
    return jnp.clip(drawn, min=-most, max=most).astype(dtype)


def setup_inputs(seed: int = 0) -> dict:
    streams_of = jax.random.split(jax.random.key(seed), 11)
    return {
        "tokens": gaussian(streams_of[0], (BATCH, TIMES, PATCHES, D), 1.0, 6.0, ((1, 16), (2, 8))),
        "grad_out": gaussian(streams_of[1], (BATCH, TIMES, PATCHES, D), 1.0, 6.0, ((1, 16), (2, 8))),
        "temporal_query": draw_temporal_query(jax.random.fold_in(streams_of[10], 71), 0),
        "temporal_key": draw_temporal_key(jax.random.fold_in(streams_of[10], 71), 0),
        "temporal_value": gaussian(streams_of[4], (D, HW), D ** -0.5, 0.15625),
        "temporal_out": gaussian(streams_of[5], (HW, D), HW ** -0.5, 0.21875),
        "spatial_query": draw_spatial_query(jax.random.fold_in(streams_of[10], 71), 0),
        "spatial_key": draw_spatial_key(jax.random.fold_in(streams_of[10], 71), 0),
        "spatial_value": gaussian(streams_of[8], (D, HW), D ** -0.5, 0.15625),
        "spatial_out": gaussian(streams_of[9], (HW, D), HW ** -0.5, 0.21875),
    }


EPSILON = 1e-05
TEMPORAL = ('blghe', 'bmghe')
SPATIAL = ('bglhe', 'bgmhe')

def layer_stats(values):
    centre = lax.optimization_barrier(jnp.mean(values, axis=-1, keepdims=True))
    spread = lax.optimization_barrier(jnp.mean(jnp.square(values - centre), axis=-1, keepdims=True))
    inverse = lax.rsqrt(spread + EPSILON)
    return ((values - centre) * inverse, inverse)

def norm_grad(normed, inverse, upstream):
    first_mean = lax.optimization_barrier(jnp.mean(upstream, axis=-1, keepdims=True))
    cross_mean = lax.optimization_barrier(jnp.mean(upstream * normed, axis=-1, keepdims=True))
    return inverse * (upstream - first_mean - normed * cross_mean)

def project(inputs, weight):
    joined = inputs.reshape(-1, inputs.shape[-1])
    result = jnp.dot(joined, weight, preferred_element_type=jnp.float32).astype(jnp.bfloat16)
    return result.reshape(inputs.shape[:-1] + (weight.shape[1],))

def back_project(members, weights):
    summed = None
    for member, weight in zip(members, weights):
        joined = member.reshape(-1, HEADS * HD)
        term = jnp.dot(joined, weight.T, preferred_element_type=jnp.float32)
        summed = term if summed is None else summed + term
    return summed.astype(jnp.bfloat16).reshape(members[0].shape[:-2] + (weights[0].shape[0],))

def split_heads(values):
    return values.reshape(values.shape[:-1] + (HEADS, HD))

def merge_heads(values):
    return values.reshape(values.shape[:-2] + (HEADS * HD,))

def product(einsum_form, left, right):
    return jnp.einsum(einsum_form, left.astype(jnp.float32), right.astype(jnp.float32))

def score_table(queries, key_rows, pattern):
    return product(pattern[0] + ',' + pattern[1] + '->bghlm', queries, key_rows) * HD ** (-0.5)

def attend(queries, key_rows, value_rows, pattern):
    scores = score_table(queries, key_rows, pattern)
    row_top = lax.optimization_barrier(jnp.max(scores, axis=-1, keepdims=True))
    logsum = row_top[..., 0] + jnp.log(lax.optimization_barrier(jnp.sum(jnp.exp(scores - row_top), axis=-1)))
    shares = jnp.exp(scores - logsum[..., None]).astype(jnp.bfloat16)
    blended = product('bghlm,' + pattern[1] + '->' + pattern[0], shares, value_rows).astype(jnp.bfloat16)
    return (blended, logsum)

def offsets(grad_mix, blended, pattern):
    return product(pattern[0] + ',' + pattern[0] + '->bghl', grad_mix, blended)

def score_grads(queries, key_rows, value_rows, grad_mix, logsum, offset, pattern):
    scores = score_table(queries, key_rows, pattern)
    shares = jnp.exp(scores - logsum[..., None])
    grad_shares = product(pattern[0] + ',' + pattern[1] + '->bghlm', grad_mix, value_rows)
    grad_scores = (shares * (grad_shares - offset[..., None]) * HD ** (-0.5)).astype(jnp.bfloat16)
    return (shares.astype(jnp.bfloat16), grad_scores)

def attention_grads(queries, key_rows, value_rows, grad_mix, pattern):
    blended, logsum = attend(queries, key_rows, value_rows, pattern)
    offset = offsets(grad_mix, blended, pattern)
    shares, grad_scores = score_grads(queries, key_rows, value_rows, grad_mix, logsum, offset, pattern)
    grad_query = product('bghlm,' + pattern[1] + '->' + pattern[0], grad_scores, key_rows).astype(jnp.bfloat16)
    key_form = 'bghlm,' + pattern[0] + '->' + pattern[1]
    grad_key = product(key_form, grad_scores, queries).astype(jnp.bfloat16)
    grad_value = product(key_form, shares, grad_mix).astype(jnp.bfloat16)
    return (grad_query, grad_key, grad_value)

def spatial_slice(operands):
    queries, key_rows, value_rows, grad_mix = [member[:, None] for member in operands]
    grads = attention_grads(queries, key_rows, value_rows, grad_mix, SPATIAL)
    return tuple((member[:, 0] for member in grads))

def reference(tokens, grad_out, temporal_query, temporal_key, temporal_value, temporal_out, spatial_query, spatial_key, spatial_value, spatial_out):
    source = tokens.astype(jnp.float32)
    normed_in, inverse_in = layer_stats(source)
    first_rows = normed_in.astype(jnp.bfloat16)
    time_query = split_heads(project(first_rows, temporal_query))
    time_key = split_heads(project(first_rows, temporal_key))
    time_value = split_heads(project(first_rows, temporal_value))
    time_blend, time_logsum = attend(time_query, time_key, time_value, TEMPORAL)
    time_branch = project(merge_heads(time_blend), temporal_out)
    middle = source + time_branch.astype(jnp.float32)
    normed_mid, inverse_mid = layer_stats(middle)
    second_rows = normed_mid.astype(jnp.bfloat16)
    space_query = split_heads(project(second_rows, spatial_query))
    space_key = split_heads(project(second_rows, spatial_key))
    space_value = split_heads(project(second_rows, spatial_value))
    space_grad_mix = split_heads(project(grad_out, spatial_out.T))
    stacked = tuple((jnp.moveaxis(member, 1, 0) for member in (space_query, space_key, space_value, space_grad_mix)))
    mapped = lax.map(spatial_slice, stacked)
    space_grads = tuple((jnp.moveaxis(member, 0, 1) for member in mapped))
    grad_second = back_project(space_grads, (spatial_query, spatial_key, spatial_value))
    grad_mid = (grad_out.astype(jnp.float32) + norm_grad(normed_mid, inverse_mid, grad_second.astype(jnp.float32))).astype(jnp.bfloat16)
    time_grad_mix = split_heads(project(grad_mid, temporal_out.T))
    time_grads = attention_grads(time_query, time_key, time_value, time_grad_mix, TEMPORAL)
    grad_first = back_project(time_grads, (temporal_query, temporal_key, temporal_value))
    return (grad_mid.astype(jnp.float32) + norm_grad(normed_in, inverse_in, grad_first.astype(jnp.float32))).astype(jnp.bfloat16)
```

```python
import jax
import jax.numpy as jnp
from jax import lax
from jax.sharding import PartitionSpec as P

HEADS = 6
HD = 128
SLOTS = 8
EPSILON = 1e-05
SCALE = HD ** (-0.5)
BF = jnp.bfloat16
F32 = jnp.float32


def layer_stats(values):
    centre = jnp.mean(values, axis=-1, keepdims=True)
    spread = jnp.mean(jnp.square(values - centre), axis=-1, keepdims=True)
    inverse = lax.rsqrt(spread + EPSILON)
    return ((values - centre) * inverse, inverse)


def norm_grad(normed, inverse, upstream):
    first_mean = jnp.mean(upstream, axis=-1, keepdims=True)
    cross_mean = jnp.mean(upstream * normed, axis=-1, keepdims=True)
    return inverse * (upstream - first_mean - normed * cross_mean)


def mm(left, right):
    return jnp.dot(left, right, preferred_element_type=F32)


def mmt(left, right):
    return lax.dot_general(left, right, (((1,), (1,)), ((), ())), preferred_element_type=F32)


def ein(form, left, right):
    return jnp.einsum(form, left, right, preferred_element_type=F32)


def forward(query, key, value, mask):
    scores = ein("glx,gmx->glm", query, key) * SCALE
    if mask is not None:
        scores = jnp.where(mask, scores, -jnp.inf)
    top = jnp.max(scores, axis=-1, keepdims=True)
    grown = jnp.exp(scores - top)
    shares = grown / jnp.sum(grown, axis=-1, keepdims=True)
    blend = ein("glm,gmx->glx", shares.astype(BF), value).astype(BF)
    return shares, blend


def backward(query, key, value, shares, blend, mix):
    offset = jnp.sum(mix.astype(F32) * blend.astype(F32), axis=-1, keepdims=True)
    grad_scores = (shares * (ein("glx,gmx->glm", mix, value) - offset) * SCALE).astype(BF)
    grad_query = ein("glm,gmx->glx", grad_scores, key).astype(BF)
    grad_key = ein("glm,glx->gmx", grad_scores, query).astype(BF)
    grad_value = ein("glm,glx->gmx", shares.astype(BF), mix).astype(BF)
    return grad_query, grad_key, grad_value


def to_time(rows):
    width = rows.shape[-1]
    moved = lax.all_to_all(rows.reshape(2, 128, width), "tm", 1, 0, tiled=True)
    return moved.reshape(256, width)


def to_home(rows):
    width = rows.shape[-1]
    moved = lax.all_to_all(rows.reshape(32, 8, width), "tm", 0, 1, tiled=True)
    return moved.reshape(256, width)


def heads_first(rows):
    return rows.reshape(256, HEADS, HD).transpose(1, 0, 2)


def heads_last(heads):
    return heads.transpose(1, 0, 2).reshape(256, HEADS * HD)


def to_heads(members):
    stacked = jnp.stack([heads_first(m) for m in members], axis=1)
    padded = jnp.pad(stacked, ((0, SLOTS - HEADS), (0, 0), (0, 0), (0, 0)))
    moved = lax.all_to_all(padded, "space", 0, 0, tiled=True)
    moved = moved.reshape(8, len(members), 2, 128, HD).transpose(1, 2, 0, 3, 4)
    return moved.reshape(len(members), 2, 1024, HD)


def from_heads(members):
    count = len(members)
    stacked = jnp.stack(members, axis=0).reshape(count, 2, 8, 128, HD).transpose(2, 0, 1, 3, 4)
    moved = lax.all_to_all(stacked, "space", 0, 0, tiled=True)
    kept = moved[:HEADS].reshape(HEADS, count, 256, HD)
    return [heads_last(kept[:, i]) for i in range(count)]


def on_device(tokens, grad_out, tq, tk, tv, to, sq, sk, sv, so):
    tokens = tokens.reshape(256, 1536)
    grad_out = grad_out.reshape(256, 1536)
    space_mix = mmt(grad_out, so).astype(BF)
    source = to_time(tokens).astype(F32)
    first_rows = layer_stats(source)[0].astype(BF)
    query, key, value = (heads_first(mm(first_rows, w).astype(BF)) for w in (tq, tk, tv))
    place = jnp.arange(256) % 8
    mask = (place[:, None] == place[None, :])[None]
    shares, blend = forward(query, key, value, mask)
    home_blend = to_home(heads_last(blend))
    branch = mm(home_blend, to).astype(BF)
    middle = tokens.astype(F32) + branch.astype(F32)
    normed_mid, inverse_mid = layer_stats(middle)
    second_rows = normed_mid.astype(BF)
    members = [mm(second_rows, w).astype(BF) for w in (sq, sk, sv)] + [space_mix]
    squery, skey, svalue, smix = to_heads(members)
    sshares, sblend = forward(squery, skey, svalue, None)
    grads = from_heads(backward(squery, skey, svalue, sshares, sblend, smix))
    grad_second = sum(mmt(g, w) for g, w in zip(grads, (sq, sk, sv))).astype(BF)
    grad_mid = (
        grad_out.astype(F32) + norm_grad(normed_mid, inverse_mid, grad_second.astype(F32))
    ).astype(BF)
    mix = heads_first(to_time(mmt(grad_mid, to).astype(BF)))
    tgrads = [heads_last(g) for g in backward(query, key, value, shares, blend, mix)]
    grad_first = to_home(sum(mmt(g, w) for g, w in zip(tgrads, (tq, tk, tv))).astype(BF))
    normed_in, inverse_in = layer_stats(tokens.astype(F32))
    grad_in = grad_mid.astype(F32) + norm_grad(normed_in, inverse_in, grad_first.astype(F32))
    return grad_in.astype(BF).reshape(1, 2, 128, 1536)


def solution(mesh):
    row = P(None, "tm", "space", None)
    return jax.shard_map(
        on_device,
        mesh=mesh,
        in_specs=(row, row) + (P(),) * 8,
        out_specs=row,
        check_vma=False,
    )
```

```python
import math

import jax
import jax.numpy as jnp
from jax import lax
from jax.experimental import pallas as pl
from jax.experimental.pallas import tpu as pltpu
from jax.sharding import PartitionSpec as P

EPSILON = 1e-05
SCALE = 128 ** (-0.5)
SCALE2 = SCALE * math.log2(math.e)
BF = jnp.bfloat16
F32 = jnp.float32
D = 1536
HW = 768
MESH = pl.DeviceIdType.MESH


def mm(left, right):
    return jnp.dot(left, right, preferred_element_type=F32)


def mmt(left, right):
    return lax.dot_general(left, right, (((1,), (1,)), ((), ())), preferred_element_type=F32)


def tmm(left, right):
    return lax.dot_general(left, right, (((0,), (0,)), ((), ())), preferred_element_type=F32)


def mean(rows):
    return jnp.sum(rows, axis=-1, keepdims=True) * (1.0 / D)


def layer_stats(rows):
    centred = rows - mean(rows)
    inverse = lax.rsqrt(mean(centred * centred) + EPSILON)
    return centred * inverse, inverse


def norm_grad(normed, inverse, upstream):
    return inverse * (upstream - mean(upstream) - normed * mean(upstream * normed))


def rows16(ref, i):
    part = ref[i // 8, pl.ds((i % 8) * 2, 2)]
    return part.astype(F32).reshape(16, part.shape[-1])


def kernel(
    tok, gout, tq, tk, tv, to, sq, sk, sv, so,
    out,
    w_tq, w_tk, w_tv, w_to, w_sq, w_sk, w_sv, w_so,
    tok_h, gout_v, tok_t, nin, iin, rows_b, q_t, k_t, v_t, p_t, b_t,
    blend_s, blend_h, wide, nmid, imid,
    k_s, v_s, q_s, g_s, k_l, v_l, q_l, g_l,
    gq_a, gk_f, gv_f, gk_a, gv_a, gq_l, gk_l, gv_l,
    acc, gmid, mix_s, mix_l, tg, first_s, first_l,
    load_sem, tm_send, tm_recv, sp_send, sp_recv, back_send, back_recv,
):
    me_t = lax.axis_index("tm")
    me_s = lax.axis_index("space")

    loads = [
        pltpu.make_async_copy(src, dst, load_sem.at[n])
        for n, (src, dst) in enumerate((
            (gout, gout_v), (so, w_so), (tok, tok_h), (tq, w_tq), (tk, w_tk), (tv, w_tv),
            (to, w_to), (sk, w_sk), (sv, w_sv), (sq, w_sq),
        ))
    ]
    for load in loads:
        load.start()

    barrier = pltpu.get_barrier_semaphore()

    def greet_t(k, c):
        pl.semaphore_signal(barrier, 1, device_id={"tm": (me_t + k) % 16}, device_id_type=MESH)
        return c

    def greet_s(k, c):
        pl.semaphore_signal(barrier, 1, device_id={"space": (me_s + k) % 8}, device_id_type=MESH)
        return c

    lax.fori_loop(1, 16, greet_t, 0)
    lax.fori_loop(1, 8, greet_s, 0)
    pl.semaphore_wait(barrier, 22)

    def tm_copy(phase, src, dst, peer):
        return pltpu.make_async_remote_copy(
            src_ref=src, dst_ref=dst, send_sem=tm_send.at[phase, peer], recv_sem=tm_recv.at[phase, me_t],
            device_id={"tm": peer}, device_id_type=MESH)

    def time_part(ref, n):
        return ref.at[pl.ds(2 * n, 2)]

    def home_part(ref, n):
        return ref.at[:, n]

    def tm_start(phase, src, src_part, dst, dst_part):
        pltpu.make_async_copy(src_part(src, me_t), dst_part(dst, me_t), tm_recv.at[phase, me_t]).start()

        def go(k, c):
            peer = (me_t + k) % 16
            tm_copy(phase, src_part(src, peer), dst_part(dst, me_t), peer).start()
            return c

        lax.fori_loop(1, 16, go, 0)

    def tm_wait(phase, dst, dst_part):
        def go(n, c):
            part = dst_part(dst, n)
            pltpu.make_async_copy(part, part, tm_recv.at[phase, n]).wait()
            return c

        lax.fori_loop(0, 16, go, 0)

    def tm_sent(phase, src, src_part, dst, dst_part):
        def go(k, c):
            peer = (me_t + k) % 16
            tm_copy(phase, src_part(src, peer), dst_part(dst, me_t), peer).wait_send()
            return c

        lax.fori_loop(1, 16, go, 0)

    def slab(ref, n, whole, rows):
        if whole:
            return ref.at[n // 4, n % 4]
        half = 4 + (n % 4) // 2
        if rows == 128:
            return ref.at[n // 4, half]
        return ref.at[n // 4, half, pl.ds(pl.multiple_of((n % 2) * 64, 64), 64)]

    def stripe(ref, n, whole, rows):
        if len(ref.shape) == 3:
            return ref.at[0 if whole else 1, pl.ds(pl.multiple_of(n * 128, 128), 128)]
        if whole:
            return ref.at[pl.ds(pl.multiple_of(n * 128, 128), 128)]
        return ref.at[pl.ds(pl.multiple_of(1024 + n * 64, 64), 64)]

    def sp_copies(which, src, dst, peer, rows):
        return [
            pltpu.make_async_remote_copy(
                src_ref=slab(src, peer, whole, rows), dst_ref=stripe(dst, me_s, whole, rows),
                send_sem=sp_send.at[which, kind, peer], recv_sem=sp_recv.at[which, kind, me_s],
                device_id={"space": peer}, device_id_type=MESH)
            for kind, whole in enumerate((True, False))
        ]

    def sp_start(which, src, dst, rows):
        for kind, whole in enumerate((True, False)):
            pltpu.make_async_copy(
                slab(src, me_s, whole, rows), stripe(dst, me_s, whole, rows), sp_recv.at[which, kind, me_s]
            ).start()

        def go(k, c):
            for copy in sp_copies(which, src, dst, (me_s + k) % 8, rows):
                copy.start()
            return c

        lax.fori_loop(1, 8, go, 0)

    def sp_wait(which, dst, rows):
        def go(n, c):
            for kind, whole in enumerate((True, False)):
                part = stripe(dst, n, whole, rows)
                pltpu.make_async_copy(part, part, sp_recv.at[which, kind, n]).wait()
            return c

        lax.fori_loop(0, 8, go, 0)

    def sp_sent(which, src, dst, rows):
        def go(k, c):
            for copy in sp_copies(which, src, dst, (me_s + k) % 8, rows):
                copy.wait_send()
            return c

        lax.fori_loop(1, 8, go, 0)

    def home_slot(ref, n, whole, rows):
        if whole:
            return ref.at[n // 4, n % 4]
        if rows == 64:
            return ref.at[n // 4, 4 + (n % 4) // 2, pl.ds(pl.multiple_of((n % 2) * 64, 64), 64)]
        return ref.at[n // 4, 4 + n % 4]

    def back_copies(which, src, dst, peer, rows):
        return [
            pltpu.make_async_remote_copy(
                src_ref=stripe(src, peer, whole, rows), dst_ref=home_slot(dst, me_s, whole, rows),
                send_sem=back_send.at[which, kind, peer], recv_sem=back_recv.at[which, kind, me_s],
                device_id={"space": peer}, device_id_type=MESH)
            for kind, whole in enumerate((True, False))
        ]

    def back_start(which, src, dst, rows):
        for kind, whole in enumerate((True, False)):
            pltpu.make_async_copy(
                stripe(src, me_s, whole, rows), home_slot(dst, me_s, whole, rows), back_recv.at[which, kind, me_s]
            ).start()

        def go(k, c):
            for copy in back_copies(which, src, dst, (me_s + k) % 8, rows):
                copy.start()
            return c

        lax.fori_loop(1, 8, go, 0)

    def back_wait(which, dst, rows):
        def go(n, c):
            for kind, whole in enumerate((True, False)):
                part = home_slot(dst, n, whole, rows)
                pltpu.make_async_copy(part, part, back_recv.at[which, kind, n]).wait()
            return c

        lax.fori_loop(0, 8, go, 0)

    def back_sent(which, src, dst, rows):
        def go(k, c):
            for copy in back_copies(which, src, dst, (me_s + k) % 8, rows):
                copy.wait_send()
            return c

        lax.fori_loop(1, 8, go, 0)

    def put_heads(ref, flat):
        for t in range(2):
            for h in range(6):
                ref[t, h] = flat[t * 128:(t + 1) * 128, h * 128:(h + 1) * 128]

    tm_start(0, tok, home_part, tok_t, time_part)

    loads[0].wait()
    loads[1].wait()
    put_heads(g_s, mmt(gout_v[...], w_so[...]).astype(BF))
    sp_start(3, g_s, g_l, 64)

    loads[2].wait()

    def norm_home(i, c):
        normed, inverse = layer_stats(rows16(tok_h, i))
        at = pl.ds(pl.multiple_of(i * 16, 16), 16)
        nin[at] = normed
        iin[at] = inverse
        return c

    lax.fori_loop(0, 16, norm_home, 0)

    tm_wait(0, tok_t, time_part)

    def norm_time(i, c):
        normed, _ = layer_stats(tok_t[pl.ds(i * 2, 2)].astype(F32).reshape(16, D))
        rows_b[pl.ds(pl.multiple_of(i * 16, 16), 16)] = normed.astype(BF)
        return c

    lax.fori_loop(0, 16, norm_time, 0)
    for n, (weight, dst) in enumerate(((w_tq, q_t), (w_tk, k_t), (w_tv, v_t))):
        loads[3 + n].wait()
        flat = mm(rows_b[...], weight[...]).astype(BF)
        for h in range(6):
            dst[h] = flat[:, h * 128:(h + 1) * 128]

    patch_q = lax.broadcasted_iota(jnp.int32, (256, 256), 0) % 8
    patch_k = lax.broadcasted_iota(jnp.int32, (256, 256), 1) % 8
    same = patch_q == patch_k

    for h in range(6):
        scores = jnp.where(same, mmt(q_t[h], k_t[h]), -jnp.inf)
        grown = jnp.exp2((scores - jnp.max(scores, axis=-1, keepdims=True)) * SCALE2)
        shares = grown * (1.0 / jnp.sum(grown, axis=-1, keepdims=True))
        p_t[h] = shares
        blend = mm(shares.astype(BF), v_t[h])
        b_t[h] = blend.astype(BF)
        blend_s[:, :, h * 128:(h + 1) * 128] = blend.reshape(32, 8, 128).astype(BF)
    tm_start(1, blend_s, time_part, blend_h, home_part)

    loads[6].wait()
    tm_wait(1, blend_h, home_part)
    home = blend_h[...].astype(F32).reshape(256, HW).astype(BF)
    wide[...] = mm(home, w_to[...]).astype(BF)

    def norm_mid(i, c):
        at = pl.ds(pl.multiple_of(i * 16, 16), 16)
        normed, inverse = layer_stats(rows16(tok_h, i) + wide[at].astype(F32))
        nmid[at] = normed
        imid[at] = inverse
        rows_b[at] = normed.astype(BF)
        return c

    lax.fori_loop(0, 16, norm_mid, 0)
    for n, (weight, src, dst, rows) in enumerate((
        (w_sk, k_s, k_l, 128), (w_sv, v_s, v_l, 128), (w_sq, q_s, q_l, 64),
    )):
        loads[7 + n].wait()
        put_heads(src, mm(rows_b[...], weight[...]).astype(BF))
        sp_start(n, src, dst, rows)

    sp_wait(3, g_l, 64)
    sp_wait(0, k_l, 128)
    sp_wait(1, v_l, 128)
    sp_wait(2, q_l, 64)
    gk_f[...] = jnp.zeros_like(gk_f)
    gv_f[...] = jnp.zeros_like(gv_f)

    def attend(i, c):
        u = i // 4
        at = pl.ds(pl.multiple_of(i * 256, 256), 256)
        query, mix, key, value = q_l[at], g_l[at], k_l[u], v_l[u]
        scores = mmt(query, key)
        grown = jnp.exp2((scores - jnp.max(scores, axis=-1, keepdims=True)) * SCALE2)
        shares = grown * (1.0 / jnp.sum(grown, axis=-1, keepdims=True))
        rounded = shares.astype(BF)
        blend = mm(rounded, value).astype(BF)
        offset = jnp.sum(mix.astype(F32) * blend.astype(F32), axis=-1, keepdims=True)
        grads = (shares * (mmt(mix, value) - offset) * SCALE).astype(BF)
        gq_a[at] = mm(grads, key).astype(BF)
        gk_f[u] += tmm(grads, query)
        gv_f[u] += tmm(rounded, mix)
        return c

    lax.fori_loop(0, 6, attend, 0)
    back_start(0, gq_a, gq_l, 64)
    gk_a[...] = gk_f[...].astype(BF)
    back_start(1, gk_a, gk_l, 128)
    gv_a[...] = gv_f[...].astype(BF)
    back_start(2, gv_a, gv_l, 128)

    def take(ref, h):
        return ref[:, h].reshape(256, 128)

    def joined(ref):
        parts = [take(ref, h) for h in range(4)]
        for h in (4, 6):
            parts.append((take(ref, h).astype(F32) + take(ref, h + 1).astype(F32)).astype(BF))
        return jnp.concatenate(parts, axis=-1)

    back_wait(0, gq_l, 64)
    acc[...] = mmt(jnp.concatenate([take(gq_l, h) for h in range(6)], axis=-1), w_sq[...])
    back_wait(1, gk_l, 128)
    acc[...] += mmt(joined(gk_l), w_sk[...])
    back_wait(2, gv_l, 128)
    acc[...] += mmt(joined(gv_l), w_sv[...])

    def grad_norm_mid(i, c):
        at = pl.ds(pl.multiple_of(i * 16, 16), 16)
        upstream = acc[at].astype(BF).astype(F32)
        grad = norm_grad(nmid[at], imid[at], upstream)
        gmid[at] = (gout_v[at].astype(F32) + grad).astype(BF)
        return c

    lax.fori_loop(0, 16, grad_norm_mid, 0)
    mix_s[...] = mmt(gmid[...], w_to[...]).reshape(2, 16, 8, HW).astype(BF)
    tm_start(2, mix_s, home_part, mix_l, time_part)
    tm_wait(2, mix_l, time_part)

    for h in range(6):
        cols = pl.ds(h * 128, 128)
        mix = mix_l[:, :, cols].astype(F32).reshape(256, 128)
        offset = jnp.sum(mix * b_t[h].astype(F32), axis=-1, keepdims=True)
        mix = mix.astype(BF)
        shares = p_t[h]
        grads = (shares * (mmt(mix, v_t[h]) - offset) * SCALE).astype(BF)
        tg[0, :, cols] = mm(grads, k_t[h]).astype(BF)
        tg[1, :, cols] = tmm(grads, q_t[h]).astype(BF)
        tg[2, :, cols] = tmm(shares.astype(BF), mix).astype(BF)
    acc[...] = mmt(tg[0], w_tq[...])
    acc[...] += mmt(tg[1], w_tk[...])
    acc[...] += mmt(tg[2], w_tv[...])
    first_s[...] = acc[...].reshape(32, 8, D).astype(BF)
    tm_start(3, first_s, time_part, first_l, home_part)
    tm_wait(3, first_l, home_part)

    def grad_norm_in(i, c):
        at = pl.ds(pl.multiple_of(i * 16, 16), 16)
        grad = norm_grad(nin[at], iin[at], rows16(first_l, i))
        out[at] = (gmid[at].astype(F32) + grad).astype(BF)
        return c

    lax.fori_loop(0, 16, grad_norm_in, 0)

    tm_sent(0, tok, home_part, tok_t, time_part)
    tm_sent(1, blend_s, time_part, blend_h, home_part)
    tm_sent(2, mix_s, home_part, mix_l, time_part)
    tm_sent(3, first_s, time_part, first_l, home_part)
    sp_sent(3, g_s, g_l, 64)
    sp_sent(0, k_s, k_l, 128)
    sp_sent(1, v_s, v_l, 128)
    sp_sent(2, q_s, q_l, 64)
    back_sent(0, gq_a, gq_l, 64)
    back_sent(1, gk_a, gk_l, 128)
    back_sent(2, gv_a, gv_l, 128)


def on_device(tokens, grad_out, *weights):
    bf = lambda *shape: pltpu.VMEM(shape, BF)
    f32 = lambda *shape: pltpu.VMEM(shape, F32)
    dma = pltpu.SemaphoreType.DMA
    tall, flat = bf(D, HW), bf(HW, D)
    any_space = pl.BlockSpec(memory_space=pl.ANY)
    out = pl.pallas_call(
        kernel,
        out_shape=jax.ShapeDtypeStruct((256, D), BF),
        in_specs=[any_space] * 10,
        out_specs=pl.BlockSpec(memory_space=pltpu.VMEM),
        scratch_shapes=[
            tall, tall, tall, flat, tall, tall, tall, flat,
            bf(2, 16, 8, D), bf(256, D), bf(32, 8, D), f32(256, D), f32(256, 1), bf(256, D),
            bf(6, 256, 128), bf(6, 256, 128), bf(6, 256, 128), f32(6, 256, 256), bf(6, 256, 128),
            bf(32, 8, HW), bf(2, 16, 8, HW), bf(256, D), f32(256, D), f32(256, 1),
            bf(2, 6, 128, 128), bf(2, 6, 128, 128), bf(2, 6, 128, 128), bf(2, 6, 128, 128),
            bf(2, 1024, 128), bf(2, 1024, 128), bf(1536, 128), bf(1536, 128),
            bf(1536, 128), f32(2, 1024, 128), f32(2, 1024, 128), bf(2, 1024, 128), bf(2, 1024, 128),
            bf(2, 6, 128, 128), bf(2, 8, 128, 128), bf(2, 8, 128, 128),
            f32(256, D), bf(256, D), bf(2, 16, 8, HW), bf(32, 8, HW), bf(3, 256, HW),
            bf(32, 8, D), bf(2, 16, 8, D),
            dma((10,)), dma((4, 16)), dma((4, 16)), dma((4, 2, 8)), dma((4, 2, 8)), dma((3, 2, 8)), dma((3, 2, 8)),
        ],
        compiler_params=pltpu.CompilerParams(
            collective_id=0, has_side_effects=True, vmem_limit_bytes=60 * 2**20
        ),
    )(tokens.reshape(2, 16, 8, D), grad_out.reshape(256, D), *weights)
    return out.reshape(1, 2, 128, D)


def solution(mesh):
    row = P(None, "tm", "space", None)
    return jax.shard_map(
        on_device,
        mesh=mesh,
        in_specs=(row, row) + (P(),) * 8,
        out_specs=row,
        check_vma=False,
    )
```

```python
import math

import jax
import jax.numpy as jnp
from jax import lax
from jax.experimental import pallas as pl
from jax.experimental.pallas import tpu as pltpu
from jax.sharding import PartitionSpec as P

EPSILON = 1e-05
SCALE = 128 ** (-0.5)
SCALE2 = SCALE * math.log2(math.e)
BF = jnp.bfloat16
F32 = jnp.float32
D = 1536
HW = 768
MESH = pl.DeviceIdType.MESH
BOTH = ((0, True), (1, False))
WHOLE, HALF = BOTH[:1], BOTH[1:]


def mm(left, right):
    return jnp.dot(left, right, preferred_element_type=F32)


def mmt(left, right):
    return lax.dot_general(left, right, (((1,), (1,)), ((), ())), preferred_element_type=F32)


def tmm(left, right):
    return lax.dot_general(left, right, (((0,), (0,)), ((), ())), preferred_element_type=F32)


def mean(rows):
    return jnp.sum(rows, axis=-1, keepdims=True) * (1.0 / D)


def layer_stats(rows):
    centred = rows - mean(rows)
    inverse = lax.rsqrt(mean(centred * centred) + EPSILON)
    return centred * inverse, inverse


def norm_grad(normed, inverse, upstream):
    return inverse * (upstream - mean(upstream) - normed * mean(upstream * normed))


def rows16(ref, i):
    part = ref[i // 8, pl.ds((i % 8) * 2, 2)]
    return part.astype(F32).reshape(16, part.shape[-1])


def kernel(
    tok, gout, tq, tk, tv, to, sq, sk, sv, so,
    out,
    w_tq, w_tk, w_tv, w_to, w_sq, w_sk, w_sv, w_so,
    tok_h, gout_v, tok_t, nin, iin, rows_b, q_t, k_t, v_t, p_t, b_t,
    blend_s, blend_h, wide, nmid, imid,
    k_s, v_s, q_s, g_s, k_l, v_l, q_l, g_l,
    gq_a, gk_f, gv_f, gk_a, gv_a, gq_l, gk_l, gv_l,
    acc, gmid, mix_s, mix_l, tg, first_s, first_l,
    load_sem, tm_send, tm_recv, sp_send, sp_recv, back_send, back_recv,
):
    me_t = lax.axis_index("tm")
    me_s = lax.axis_index("space")

    loads = [
        pltpu.make_async_copy(src, dst, load_sem.at[n])
        for n, (src, dst) in enumerate((
            (gout, gout_v), (so, w_so), (tok, tok_h), (tq, w_tq), (tk, w_tk), (tv, w_tv),
            (to, w_to), (sk, w_sk), (sv, w_sv), (sq, w_sq),
        ))
    ]
    barrier = pltpu.get_barrier_semaphore()

    def greet_t(k, c):
        pl.semaphore_signal(barrier, 1, device_id={"tm": (me_t + k) % 16}, device_id_type=MESH)
        return c

    def greet_s(k, c):
        pl.semaphore_signal(barrier, 1, device_id={"space": (me_s + k) % 8}, device_id_type=MESH)
        return c

    lax.fori_loop(1, 16, greet_t, 0)
    lax.fori_loop(1, 8, greet_s, 0)
    pl.semaphore_wait(barrier, 22)

    def tm_copy(phase, src, dst, peer):
        return pltpu.make_async_remote_copy(
            src_ref=src, dst_ref=dst, send_sem=tm_send.at[phase, peer], recv_sem=tm_recv.at[phase, me_t],
            device_id={"tm": peer}, device_id_type=MESH)

    def time_part(ref, n):
        return ref.at[pl.ds(2 * n, 2)]

    def home_part(ref, n):
        return ref.at[:, n]

    def tm_start(phase, src, src_part, dst, dst_part):
        pltpu.make_async_copy(src_part(src, me_t), dst_part(dst, me_t), tm_recv.at[phase, me_t]).start()

        def go(k, c):
            peer = (me_t + k) % 16
            tm_copy(phase, src_part(src, peer), dst_part(dst, me_t), peer).start()
            return c

        lax.fori_loop(1, 16, go, 0)

    def tm_wait(phase, dst, dst_part):
        def go(n, c):
            part = dst_part(dst, n)
            pltpu.make_async_copy(part, part, tm_recv.at[phase, n]).wait()
            return c

        lax.fori_loop(0, 16, go, 0)

    def tm_sent(phase, src, src_part, dst, dst_part):
        def go(k, c):
            peer = (me_t + k) % 16
            tm_copy(phase, src_part(src, peer), dst_part(dst, me_t), peer).wait_send()
            return c

        lax.fori_loop(1, 16, go, 0)

    def slab(ref, n, whole, rows):
        if whole:
            return ref.at[n // 4, n % 4]
        half = 4 + (n % 4) // 2
        if rows == 128:
            return ref.at[n // 4, half]
        return ref.at[n // 4, half, pl.ds(pl.multiple_of((n % 2) * 64, 64), 64)]

    def stripe(ref, n, whole, rows):
        if len(ref.shape) == 3:
            return ref.at[0 if whole else 1, pl.ds(pl.multiple_of(n * 128, 128), 128)]
        if whole:
            return ref.at[pl.ds(pl.multiple_of(n * 128, 128), 128)]
        return ref.at[pl.ds(pl.multiple_of(1024 + n * 64, 64), 64)]

    def sp_copies(which, src, dst, peer, rows, kinds):
        return [
            pltpu.make_async_remote_copy(
                src_ref=slab(src, peer, whole, rows), dst_ref=stripe(dst, me_s, whole, rows),
                send_sem=sp_send.at[which, kind, peer], recv_sem=sp_recv.at[which, kind, me_s],
                device_id={"space": peer}, device_id_type=MESH)
            for kind, whole in kinds
        ]

    def sp_start(which, src, dst, rows, kinds=BOTH):
        for kind, whole in kinds:
            pltpu.make_async_copy(
                slab(src, me_s, whole, rows), stripe(dst, me_s, whole, rows), sp_recv.at[which, kind, me_s]
            ).start()

        def go(k, c):
            for copy in sp_copies(which, src, dst, (me_s + k) % 8, rows, kinds):
                copy.start()
            return c

        lax.fori_loop(1, 8, go, 0)

    def sp_wait(which, dst, rows, kinds=BOTH):
        def go(n, c):
            for kind, whole in kinds:
                part = stripe(dst, n, whole, rows)
                pltpu.make_async_copy(part, part, sp_recv.at[which, kind, n]).wait()
            return c

        lax.fori_loop(0, 8, go, 0)

    def sp_sent(which, src, dst, rows, kinds=BOTH):
        def go(k, c):
            for copy in sp_copies(which, src, dst, (me_s + k) % 8, rows, kinds):
                copy.wait_send()
            return c

        lax.fori_loop(1, 8, go, 0)

    def home_slot(ref, n, whole, rows):
        if whole:
            return ref.at[n // 4, n % 4]
        if rows == 64:
            return ref.at[n // 4, 4 + (n % 4) // 2, pl.ds(pl.multiple_of((n % 2) * 64, 64), 64)]
        return ref.at[n // 4, 4 + n % 4]

    def back_copies(which, src, dst, peer, rows, kinds):
        return [
            pltpu.make_async_remote_copy(
                src_ref=stripe(src, peer, whole, rows), dst_ref=home_slot(dst, me_s, whole, rows),
                send_sem=back_send.at[which, kind, peer], recv_sem=back_recv.at[which, kind, me_s],
                device_id={"space": peer}, device_id_type=MESH)
            for kind, whole in kinds
        ]

    def back_start(which, src, dst, rows, kinds=BOTH):
        for kind, whole in kinds:
            pltpu.make_async_copy(
                stripe(src, me_s, whole, rows), home_slot(dst, me_s, whole, rows), back_recv.at[which, kind, me_s]
            ).start()

        def go(k, c):
            for copy in back_copies(which, src, dst, (me_s + k) % 8, rows, kinds):
                copy.start()
            return c

        lax.fori_loop(1, 8, go, 0)

    def back_wait(which, dst, rows, kinds=BOTH):
        def go(n, c):
            for kind, whole in kinds:
                part = home_slot(dst, n, whole, rows)
                pltpu.make_async_copy(part, part, back_recv.at[which, kind, n]).wait()
            return c

        lax.fori_loop(0, 8, go, 0)

    def back_sent(which, src, dst, rows, kinds=BOTH):
        def go(k, c):
            for copy in back_copies(which, src, dst, (me_s + k) % 8, rows, kinds):
                copy.wait_send()
            return c

        lax.fori_loop(1, 8, go, 0)

    def put_heads(ref, flat):
        for t in range(2):
            for h in range(6):
                ref[t, h] = flat[t * 128:(t + 1) * 128, h * 128:(h + 1) * 128]

    tm_start(0, tok, home_part, tok_t, time_part)
    for load in loads:
        load.start()

    loads[0].wait()
    loads[1].wait()
    put_heads(g_s, mmt(gout_v[...], w_so[...]).astype(BF))

    loads[2].wait()

    def norm_home(i, c):
        normed, inverse = layer_stats(rows16(tok_h, i))
        at = pl.ds(pl.multiple_of(i * 16, 16), 16)
        nin[at] = normed
        iin[at] = inverse
        return c

    lax.fori_loop(0, 16, norm_home, 0)

    def norm_time(k, c):
        n = (me_t + k) % 16
        part = time_part(tok_t, n)
        pltpu.make_async_copy(part, part, tm_recv.at[0, n]).wait()
        normed, _ = layer_stats(tok_t[pl.ds(n * 2, 2)].astype(F32).reshape(16, D))
        rows_b[pl.ds(pl.multiple_of(n * 16, 16), 16)] = normed.astype(BF)
        return c

    lax.fori_loop(0, 16, norm_time, 0)
    sp_start(3, g_s, g_l, 64)
    for n, (weight, dst) in enumerate(((w_tq, q_t), (w_tk, k_t), (w_tv, v_t))):
        loads[3 + n].wait()
        flat = mm(rows_b[...], weight[...]).astype(BF)
        for h in range(6):
            dst[h] = flat[:, h * 128:(h + 1) * 128]

    patch_q = lax.broadcasted_iota(jnp.int32, (256, 256), 0) % 8
    patch_k = lax.broadcasted_iota(jnp.int32, (256, 256), 1) % 8
    same = patch_q == patch_k

    for h in range(6):
        scores = jnp.where(same, mmt(q_t[h], k_t[h]), -jnp.inf)
        grown = jnp.exp2((scores - jnp.max(scores, axis=-1, keepdims=True)) * SCALE2)
        shares = grown * (1.0 / jnp.sum(grown, axis=-1, keepdims=True))
        p_t[h] = shares
        blend = mm(shares.astype(BF), v_t[h])
        b_t[h] = blend.astype(BF)
        blend_s[:, :, h * 128:(h + 1) * 128] = blend.reshape(32, 8, 128).astype(BF)
    tm_start(1, blend_s, time_part, blend_h, home_part)

    loads[6].wait()
    tm_wait(1, blend_h, home_part)
    home = blend_h[...].astype(F32).reshape(256, HW).astype(BF)
    wide[...] = mm(home, w_to[...]).astype(BF)

    def norm_mid(i, c):
        at = pl.ds(pl.multiple_of(i * 16, 16), 16)
        normed, inverse = layer_stats(rows16(tok_h, i) + wide[at].astype(F32))
        nmid[at] = normed
        imid[at] = inverse
        rows_b[at] = normed.astype(BF)
        return c

    lax.fori_loop(0, 16, norm_mid, 0)
    for n, (weight, src, dst, rows) in enumerate((
        (w_sk, k_s, k_l, 128), (w_sv, v_s, v_l, 128), (w_sq, q_s, q_l, 64),
    )):
        loads[7 + n].wait()
        put_heads(src, mm(rows_b[...], weight[...]).astype(BF))
        sp_start(n, src, dst, rows, WHOLE)
    for n, (src, dst, rows) in enumerate(((k_s, k_l, 128), (v_s, v_l, 128), (q_s, q_l, 64))):
        sp_start(n, src, dst, rows, HALF)

    gk_f[...] = jnp.zeros_like(gk_f)
    gv_f[...] = jnp.zeros_like(gv_f)

    def attend(i, c):
        u = i // 4
        at = pl.ds(pl.multiple_of(i * 256, 256), 256)
        query, mix, key, value = q_l[at], g_l[at], k_l[u], v_l[u]
        scores = mmt(query, key)
        grown = jnp.exp2((scores - jnp.max(scores, axis=-1, keepdims=True)) * SCALE2)
        shares = grown * (1.0 / jnp.sum(grown, axis=-1, keepdims=True))
        rounded = shares.astype(BF)
        blend = mm(rounded, value).astype(BF)
        offset = jnp.sum(mix.astype(F32) * blend.astype(F32), axis=-1, keepdims=True)
        grads = (shares * (mmt(mix, value) - offset) * SCALE).astype(BF)
        gq_a[at] = mm(grads, key).astype(BF)
        gk_f[u] += tmm(grads, query)
        gv_f[u] += tmm(rounded, mix)
        return c

    for u, kinds in enumerate((WHOLE, HALF)):
        sp_wait(3, g_l, 64, kinds)
        sp_wait(0, k_l, 128, kinds)
        sp_wait(1, v_l, 128, kinds)
        sp_wait(2, q_l, 64, kinds)
        lax.fori_loop(4 * u, 4 + 2 * u, attend, 0)
        back_start(0, gq_a, gq_l, 64, kinds)
        gk_a[u] = gk_f[u].astype(BF)
        back_start(1, gk_a, gk_l, 128, kinds)
        gv_a[u] = gv_f[u].astype(BF)
        back_start(2, gv_a, gv_l, 128, kinds)

    def take(ref, h):
        return ref[:, h].reshape(256, 128)

    def added(ref, h):
        return (take(ref, h).astype(F32) + take(ref, h + 1).astype(F32)).astype(BF)

    acc[...] = jnp.zeros_like(acc)
    for which, (ref, weight) in enumerate(((gq_l, w_sq), (gk_l, w_sk), (gv_l, w_sv))):
        back_wait(which, ref, 64 if which == 0 else 128, WHOLE)
        acc[...] += mmt(jnp.concatenate([take(ref, h) for h in range(4)], axis=-1), weight[:, :512])
    for which, (ref, weight) in enumerate(((gq_l, w_sq), (gk_l, w_sk), (gv_l, w_sv))):
        back_wait(which, ref, 64 if which == 0 else 128, HALF)
        last = (take(ref, 4), take(ref, 5)) if which == 0 else (added(ref, 4), added(ref, 6))
        acc[...] += mmt(jnp.concatenate(last, axis=-1), weight[:, 512:])

    def grad_norm_mid(i, c):
        at = pl.ds(pl.multiple_of(i * 16, 16), 16)
        upstream = acc[at].astype(BF).astype(F32)
        grad = norm_grad(nmid[at], imid[at], upstream)
        gmid[at] = (gout_v[at].astype(F32) + grad).astype(BF)
        return c

    lax.fori_loop(0, 16, grad_norm_mid, 0)
    mix_s[...] = mmt(gmid[...], w_to[...]).reshape(2, 16, 8, HW).astype(BF)
    tm_start(2, mix_s, home_part, mix_l, time_part)
    tm_wait(2, mix_l, time_part)

    for h in range(6):
        cols = pl.ds(h * 128, 128)
        mix = mix_l[:, :, cols].astype(F32).reshape(256, 128)
        offset = jnp.sum(mix * b_t[h].astype(F32), axis=-1, keepdims=True)
        mix = mix.astype(BF)
        shares = p_t[h]
        grads = (shares * (mmt(mix, v_t[h]) - offset) * SCALE).astype(BF)
        tg[0, :, cols] = mm(grads, k_t[h]).astype(BF)
        tg[1, :, cols] = tmm(grads, q_t[h]).astype(BF)
        tg[2, :, cols] = tmm(shares.astype(BF), mix).astype(BF)
    for c in range(3):
        cols = slice(c * 512, (c + 1) * 512)
        part = mmt(tg[0], w_tq[cols]) + mmt(tg[1], w_tk[cols]) + mmt(tg[2], w_tv[cols])
        first_s[c] = part.reshape(32, 8, 512).astype(BF)
        tm_start(3 + c, first_s.at[c], time_part, first_l.at[c], home_part)
    for c in range(3):
        tm_wait(3 + c, first_l.at[c], home_part)

    def grad_norm_in(i, z):
        at = pl.ds(pl.multiple_of(i * 16, 16), 16)
        grad = norm_grad(nin[at], iin[at], jnp.concatenate([rows16(first_l.at[c], i) for c in range(3)], axis=-1))
        out[at] = (gmid[at].astype(F32) + grad).astype(BF)
        return z

    lax.fori_loop(0, 16, grad_norm_in, 0)

    tm_sent(0, tok, home_part, tok_t, time_part)
    tm_sent(1, blend_s, time_part, blend_h, home_part)
    tm_sent(2, mix_s, home_part, mix_l, time_part)
    for c in range(3):
        tm_sent(3 + c, first_s.at[c], time_part, first_l.at[c], home_part)
    sp_sent(3, g_s, g_l, 64)
    sp_sent(0, k_s, k_l, 128)
    sp_sent(1, v_s, v_l, 128)
    sp_sent(2, q_s, q_l, 64)
    back_sent(0, gq_a, gq_l, 64)
    back_sent(1, gk_a, gk_l, 128)
    back_sent(2, gv_a, gv_l, 128)


def on_device(tokens, grad_out, *weights):
    bf = lambda *shape: pltpu.VMEM(shape, BF)
    f32 = lambda *shape: pltpu.VMEM(shape, F32)
    dma = pltpu.SemaphoreType.DMA
    tall, flat = bf(D, HW), bf(HW, D)
    any_space = pl.BlockSpec(memory_space=pl.ANY)
    out = pl.pallas_call(
        kernel,
        out_shape=jax.ShapeDtypeStruct((256, D), BF),
        in_specs=[any_space] * 10,
        out_specs=pl.BlockSpec(memory_space=pltpu.VMEM),
        scratch_shapes=[
            tall, tall, tall, flat, tall, tall, tall, flat,
            bf(2, 16, 8, D), bf(256, D), bf(32, 8, D), f32(256, D), f32(256, 1), bf(256, D),
            bf(6, 256, 128), bf(6, 256, 128), bf(6, 256, 128), f32(6, 256, 256), bf(6, 256, 128),
            bf(32, 8, HW), bf(2, 16, 8, HW), bf(256, D), f32(256, D), f32(256, 1),
            bf(2, 6, 128, 128), bf(2, 6, 128, 128), bf(2, 6, 128, 128), bf(2, 6, 128, 128),
            bf(2, 1024, 128), bf(2, 1024, 128), bf(1536, 128), bf(1536, 128),
            bf(1536, 128), f32(2, 1024, 128), f32(2, 1024, 128), bf(2, 1024, 128), bf(2, 1024, 128),
            bf(2, 6, 128, 128), bf(2, 8, 128, 128), bf(2, 8, 128, 128),
            f32(256, D), bf(256, D), bf(2, 16, 8, HW), bf(32, 8, HW), bf(3, 256, HW),
            bf(3, 32, 8, 512), bf(3, 2, 16, 8, 512),
            dma((10,)), dma((6, 16)), dma((6, 16)), dma((4, 2, 8)), dma((4, 2, 8)), dma((3, 2, 8)), dma((3, 2, 8)),
        ],
        compiler_params=pltpu.CompilerParams(
            collective_id=0, has_side_effects=True, vmem_limit_bytes=60 * 2**20
        ),
    )(tokens.reshape(2, 16, 8, D), grad_out.reshape(256, D), *weights)
    return out.reshape(1, 2, 128, D)


def solution(mesh):
    row = P(None, "tm", "space", None)
    return jax.shard_map(
        on_device,
        mesh=mesh,
        in_specs=(row, row) + (P(),) * 8,
        out_specs=row,
        check_vma=False,
    )
```
